32 devices in a mesh: groups: 2 (over y), tensor: 4 (over z), section: 2 (over x), split: 2 (over core).
Axes of the slice: x: 2, y: 2, z: 4, core: 2. Of those that a mesh axis runs over, the one named last changes fastest.
Arguments:
- teacher_hidden: bfloat16 [1024, 16384], P(('groups', 'section', 'split'), 'tensor'), parts along dimension 0, may hold values from -60 to 60, as said below
- teacher_gain: float32 [16384], P('tensor'), may hold values from 0.1 to 1.9
- proj_weight: bfloat16 [16384, 4096], P(('tensor', 'section'), 'split'), may hold values from -0.046875 to 0.046875
- student_input: bfloat16 [1024, 4096], P(('groups', 'split'), ('tensor', 'section')), parts along dimension 0, may hold values from -6 to 6
- student_gain: bfloat16 [4096], P(('tensor', 'section')), may hold values from 0.099609375 to 1.8984375
- gate_weight: bfloat16 [4096, 14336], P(None, ('tensor', 'section')), may hold values from -0.09375 to 0.09375
- up_weight: bfloat16 [4096, 14336], P(None, ('tensor', 'section')), may hold values from -0.09375 to 0.09375
- down_weight: bfloat16 [14336, 4096], P(('tensor', 'section')), may hold values from -0.046875 to 0.046875
- block_order: int32 [256], replicated, may hold values from 0 to 255, each once
Outputs:
- grad_gate: bfloat16 [8192, 14336], P(('groups', 'split'), ('tensor', 'section')), parts along dimension 0
- grad_up: bfloat16 [8192, 14336], P(('groups', 'split'), ('tensor', 'section')), parts along dimension 0
- grad_down: bfloat16 [28672, 4096], P(('groups', 'tensor', 'section'), 'split'), parts along dimension 0
The draws below stay inside these ranges and needn't reach their ends.
There are 2 independent parts, one for each index of `groups`. The reference program is written for one: setup_inputs(seed, part) draws one part's arguments, and reference() takes and returns one part's arrays. A program takes and returns all parts, laid end to end along the dimension named above; an argument that names none is the same for every part. Nothing has to cross between parts.
Inputs may be any that keep to these rules, and one draw needn't show every extreme that they name: `teacher_hidden`: teacher hidden states; rows differ in scale.
All inputs are finite; a program needn't handle non-finite values.
Results may differ from the reference program's by a relative error of at most 0.0083.
Values may be sent and summed in bfloat16 or wider, within the bound.
No kernel may reach another device: no remote copies, remote signals or barrier semaphores. Data moves between devices by JAX's collectives and lax.ppermute only.
A program may use at most 256 MiB of HBM per device.

```python
import jax
import jax.numpy as jnp
from jax import lax

DT = 16384
D = 4096
FF = 14336
SHARD_ROWS = 256
TOKENS = 512
N_SECTION = 2
N_SPLIT = 2


def draw_teacher_hidden(key, part):
    first = jax.random.fold_in(key, 11)
    second = jax.random.fold_in(key, 23)
    scales = jnp.exp(jax.random.uniform(first, (TOKENS, 1), jnp.float32, 0.0, 2.302585))
    position = jnp.arange(DT, dtype=jnp.float32)[None, :] / DT
    columns = jnp.exp(position * 1.098612)
    values = jax.random.normal(second, (TOKENS, DT), jnp.float32) * scales * columns
    return jnp.clip(values, -60.0, 60.0).astype(jnp.bfloat16)


def block_scale(key, shape, cuts, smallest, high):
    factor_of, own = 1.0, jax.random.fold_in(key, 6)
    for dim, blocks in cuts:
        draws = jnp.exp(jax.random.uniform(jax.random.fold_in(own, dim), (blocks,), jnp.float32, smallest / len(cuts), high / len(cuts)))
        factor_of = factor_of * jnp.repeat(draws, shape[dim] // blocks).reshape([-1 if axis == dim else 1 for axis in range(len(shape))])
    return factor_of


def bell_draw(rng, dims, spread, bound, split=(), kind=jnp.bfloat16):
    factor_of = block_scale(rng, dims, split, -0.22, 0.18) if split else 1.0
    result = jax.random.normal(rng, dims, jnp.float32) * spread * factor_of
    return jnp.minimum(jnp.maximum(result, -bound), bound).astype(kind)


def setup_inputs(seed: int = 0, part: int = 0) -> dict:
    key_of = jax.random.split(jax.random.key(seed), 10)
    own_keys = jax.random.split(jax.random.fold_in(key_of[9], part), 10)
    teacher_hidden = draw_teacher_hidden(jax.random.fold_in(jax.random.fold_in(key_of[9], part), 71), part)
    teacher_gain = jnp.clip(1.0 + 0.18 * jax.random.normal(key_of[1], (DT,), jnp.float32), 0.1, 1.9)
    proj_weight = bell_draw(key_of[2], (DT, D), DT ** -0.5, 0.046875, ((0, 8), (1, 2)))
    student_input = bell_draw(own_keys[3], (TOKENS, D), 1.0, 6.0, ((0, 2), (1, 8)))
    student_gain = jnp.clip(1.0 + 0.18 * jax.random.normal(key_of[4], (D,), jnp.float32), 0.099609375, 1.8984375).astype(jnp.bfloat16)
    gate_weight = bell_draw(key_of[5], (D, FF), D ** -0.5, 0.09375, ((1, 8),))
    up_weight = bell_draw(key_of[6], (D, FF), D ** -0.5, 0.09375, ((1, 8),))
    down_weight = bell_draw(key_of[7], (FF, D), FF ** -0.5, 0.046875, ((0, 8),))
    block_order = jax.random.permutation(key_of[8], SHARD_ROWS).astype(jnp.int32)
    return {"teacher_hidden": teacher_hidden, "teacher_gain": teacher_gain, "proj_weight": proj_weight, "student_input": student_input, "student_gain": student_gain, "gate_weight": gate_weight, "up_weight": up_weight, "down_weight": down_weight, "block_order": block_order}


def reference(teacher_hidden, teacher_gain, proj_weight, student_input, student_gain, gate_weight, up_weight, down_weight, block_order):
    eps = 1e-05
    block = SHARD_ROWS // N_SECTION
    teach = teacher_hidden.astype(jnp.float32)
    mean_sq = lax.optimization_barrier(jnp.mean(teach * teach, axis=1, keepdims=True))
    teacher_normed = (teach * lax.rsqrt(mean_sq + eps) * teacher_gain).astype(jnp.bfloat16)
    target = jnp.dot(teacher_normed, proj_weight, preferred_element_type=jnp.float32)
    blocks = target.reshape(N_SECTION, N_SPLIT, block, D)
    per_shard = jnp.transpose(blocks, (1, 0, 2, 3)).reshape(N_SPLIT, SHARD_ROWS, D)
    arranged = jnp.take(per_shard, block_order.astype(jnp.int32), axis=1)
    matched = arranged.reshape(SHARD_ROWS * N_SPLIT, D)
    inputs = student_input.astype(jnp.float32)
    stu_sq = lax.optimization_barrier(jnp.mean(inputs * inputs, axis=1, keepdims=True))
    normed = (inputs * lax.rsqrt(stu_sq + eps) * student_gain.astype(jnp.float32)).astype(jnp.bfloat16)
    gate = jnp.dot(normed, gate_weight, preferred_element_type=jnp.float32)
    up = jnp.dot(normed, up_weight, preferred_element_type=jnp.float32)
    active = jax.nn.silu(gate)
    hidden = (active * up).astype(jnp.bfloat16)
    output = jnp.dot(hidden, down_weight, preferred_element_type=jnp.float32)
    difference = inputs + (output - matched)
    cotangent = (difference * (64.0 / (SHARD_ROWS * N_SPLIT))).astype(jnp.bfloat16)
    back_hidden = jnp.dot(cotangent, down_weight.T, preferred_element_type=jnp.float32)
    sigma = jax.nn.sigmoid(gate)
    d_gate = (back_hidden * up * sigma * (1.0 + gate * (1.0 - sigma))).astype(jnp.bfloat16)
    d_up = (back_hidden * active).astype(jnp.bfloat16)
    total_gate = jnp.zeros((D, FF), jnp.float32)
    total_up = jnp.zeros((D, FF), jnp.float32)
    total_down = jnp.zeros((FF, D), jnp.float32)
    for shard in range(N_SPLIT):
        low = shard * SHARD_ROWS
        high = low + SHARD_ROWS
        part_gate = jnp.dot(normed[low:high].T, d_gate[low:high], preferred_element_type=jnp.float32)
        part_up = jnp.dot(normed[low:high].T, d_up[low:high], preferred_element_type=jnp.float32)
        part_down = jnp.dot(hidden[low:high].T, cotangent[low:high], preferred_element_type=jnp.float32)
        total_gate = total_gate + part_gate.astype(jnp.bfloat16).astype(jnp.float32)
        total_up = total_up + part_up.astype(jnp.bfloat16).astype(jnp.float32)
        total_down = total_down + part_down.astype(jnp.bfloat16).astype(jnp.float32)
    return (total_gate.astype(jnp.bfloat16), total_up.astype(jnp.bfloat16), total_down.astype(jnp.bfloat16))
```

```python
import jax
import jax.numpy as jnp
from jax import lax
from jax.sharding import PartitionSpec as P


def bit_count(size):
    return size.bit_length() - 1


def phase_orders():
    section = [("section", b) for b in range(bit_count(lax.axis_size("section")))]
    tensor = [("tensor", b) for b in range(bit_count(lax.axis_size("tensor")))]
    return section + tensor, tensor[:1] + section + tensor[1:]


def phase_swap(value, moves):
    tensors, sections, cores = (lax.axis_size(a) for a in ("tensor", "section", "split"))
    pairs = []
    for t in range(tensors):
        for s in range(sections):
            for c in range(cores):
                axis, bit = moves[c]
                to_t = t ^ (1 << bit) if axis == "tensor" else t
                to_s = s ^ (1 << bit) if axis == "section" else s
                pairs.append(((t * sections + s) * cores + c, (to_t * sections + to_s) * cores + c))
    return lax.ppermute(value, ("tensor", "section", "split"), pairs)


def swapped(value, axis, bit):
    pairs = [(source, source ^ (1 << bit)) for source in range(lax.axis_size(axis))]
    return lax.ppermute(value, axis, pairs)


def on_device(
    teacher_hidden,
    teacher_gain,
    proj_weight,
    student_input,
    student_gain,
    gate_weight,
    up_weight,
    down_weight,
    block_order,
):
    eps = 1e-05
    bf16, f32 = jnp.bfloat16, jnp.float32
    tensors, sections = lax.axis_size("tensor"), lax.axis_size("section")
    core = lax.axis_index("split")
    orders = phase_orders()
    phases = list(zip(*orders))
    index = {"tensor": lax.axis_index("tensor"), "section": lax.axis_index("section")}

    def bit_of(axis, bit):
        return (index[axis] >> bit) & 1

    bits = [jnp.where(core == 0, bit_of(*a), bit_of(*b)) for a, b in phases]
    count = len(phases)

    def owned(which):
        return sum(bit_of(*axis_bit) << (count - 1 - k) for k, axis_bit in enumerate(orders[which]))

    def gathered(value):
        for k in reversed(range(count)):
            got = phase_swap(value, phases[k])
            value = jnp.where(
                bits[k] == 1,
                jnp.concatenate([got, value], axis=1),
                jnp.concatenate([value, got], axis=1),
            )
        return value

    def natural(value):
        rows, cols = value.shape
        blocks = value.reshape((rows,) + (2,) * count + (cols >> count,))
        wanted = [("tensor", b) for b in reversed(range(bit_count(tensors)))]
        wanted += [("section", b) for b in reversed(range(bit_count(sections)))]
        forms = []
        for order in orders:
            axes = [0] + [1 + order.index(w) for w in wanted] + [1 + count]
            forms.append(jnp.transpose(blocks, axes).reshape(rows, cols))
        return jnp.where(core == 0, forms[0], forms[1])

    whole_input = natural(gathered(student_input))
    whole_gain = natural(gathered(student_gain[None, :]))[0]
    own_rows, width = whole_input.shape
    half_width = width // 2

    teach_local = teacher_hidden.astype(f32)
    total_sq = jnp.sum(teach_local * teach_local, axis=1)
    for b in range(bit_count(tensors)):
        total_sq = total_sq + swapped(total_sq, "tensor", b)
    narrow = teacher_hidden.shape[1] // sections
    section = index["section"]
    if sections == 2:
        away = lax.dynamic_slice_in_dim(teacher_hidden, (1 - section) * narrow, narrow, 1)
        stay = lax.dynamic_slice_in_dim(teacher_hidden, section * narrow, narrow, 1)
        moved = jnp.concatenate([stay, swapped(away, "section", 0)], axis=0)
        total_sq = jnp.concatenate([total_sq, swapped(total_sq, "section", 0)])
        block = teacher_hidden.shape[0]
        picks = block_order ^ (section * block) if block & (block - 1) == 0 else (
            (block_order // block) ^ section
        ) * block + block_order % block
    else:
        moved = lax.all_to_all(teacher_hidden, "section", split_axis=1, concat_axis=0, tiled=True)
        total_sq = lax.all_gather(total_sq, "section", axis=0, tiled=True)
        picks = block_order
    piece_gain = lax.dynamic_slice_in_dim(teacher_gain, section * narrow, narrow, 0)
    teacher_width = narrow * tensors * sections
    scaled = moved.astype(f32) * lax.rsqrt(total_sq / teacher_width + eps)[:, None] * piece_gain
    teacher_normed = scaled.astype(bf16)
    chosen = (picks[:, None] == jnp.arange(own_rows)[None, :]).astype(bf16)
    arranged = jnp.dot(chosen, teacher_normed, preferred_element_type=f32).astype(bf16)
    arranged_pair = jnp.concatenate([arranged, swapped(arranged, "split", 0)], axis=0)
    target = jnp.dot(arranged_pair, proj_weight, preferred_element_type=f32)

    inputs = whole_input.astype(f32)
    stu_sq = jnp.mean(inputs * inputs, axis=1, keepdims=True)
    normed = (inputs * lax.rsqrt(stu_sq + eps) * whole_gain.astype(f32)).astype(bf16)
    normed_away = lax.dynamic_slice_in_dim(normed, (1 - core) * half_width, half_width, 1)
    normed_stay = lax.dynamic_slice_in_dim(normed, core * half_width, half_width, 1)
    normed_pair = jnp.concatenate([normed_stay, swapped(normed_away, "split", 0)], axis=0)
    part_cols = half_width >> count
    mine = jnp.where(core == 0, owned(0), owned(1))
    other = jnp.where(core == 0, owned(1), owned(0))
    input_stay = lax.dynamic_slice_in_dim(
        whole_input, core * half_width + mine * part_cols, part_cols, 1
    )
    input_away = lax.dynamic_slice_in_dim(
        whole_input, (1 - core) * half_width + other * part_cols, part_cols, 1
    )
    input_pair = jnp.concatenate([input_stay, swapped(input_away, "split", 0)], axis=0)
    gate = jnp.dot(normed, gate_weight, preferred_element_type=f32)
    up = jnp.dot(normed, up_weight, preferred_element_type=f32)
    active = jax.nn.silu(gate)
    hidden = (active * up).astype(bf16)
    hidden_pair = jnp.concatenate([hidden, swapped(hidden, "split", 0)], axis=0)

    down_half = lax.dynamic_slice_in_dim(down_weight, core * half_width, half_width, 1)
    current = jnp.dot(hidden_pair, down_half, preferred_element_type=f32) - target
    for k in range(count):
        half = current.shape[1] // 2
        away = lax.dynamic_slice_in_dim(current, (1 - bits[k]) * half, half, 1).astype(bf16)
        stay = lax.dynamic_slice_in_dim(current, bits[k] * half, half, 1)
        current = stay + phase_swap(away, phases[k]).astype(f32)
    total_rows = own_rows * lax.axis_size("split")
    difference = input_pair.astype(f32) + current
    cotangent_half = gathered((difference * (64.0 / total_rows)).astype(bf16))

    cot_stay, cot_away = cotangent_half[:own_rows], cotangent_half[own_rows:]
    cot_got = swapped(cot_away, "split", 0)
    cotangent = jnp.where(
        core == 0,
        jnp.concatenate([cot_stay, cot_got], axis=1),
        jnp.concatenate([cot_got, cot_stay], axis=1),
    )
    back_hidden = lax.dot_general(
        cotangent, down_weight, (((1,), (1,)), ((), ())), preferred_element_type=f32
    )
    sigma = jax.nn.sigmoid(gate)
    d_gate = (back_hidden * up * sigma * (1.0 + gate * (1.0 - sigma))).astype(bf16)
    d_up = (back_hidden * active).astype(bf16)
    got_gate, got_up = swapped((d_gate, d_up), "split", 0)
    d_gate_pair = jnp.concatenate([d_gate, got_gate], axis=0)
    d_up_pair = jnp.concatenate([d_up, got_up], axis=0)
    contract_rows = (((0,), (0,)), ((), ()))

    def over_rows(left, right):
        return lax.dot_general(left, right, contract_rows, preferred_element_type=f32).astype(bf16)

    grad_down = over_rows(hidden_pair, cotangent_half)
    grad_gate = over_rows(normed_pair, d_gate_pair)
    grad_up = over_rows(normed_pair, d_up_pair)
    return grad_gate, grad_up, grad_down


def solution(mesh):
    placed = (
        P(("groups", "section", "split"), "tensor"),
        P("tensor"),
        P(("tensor", "section"), "split"),
        P(("groups", "split"), ("tensor", "section")),
        P(("tensor", "section")),
        P(None, ("tensor", "section")),
        P(None, ("tensor", "section")),
        P(("tensor", "section"), None),
        P(),
    )
    return jax.shard_map(
        on_device,
        mesh=mesh,
        in_specs=placed,
        out_specs=(
            P(("groups", "split"), ("tensor", "section")),
            P(("groups", "split"), ("tensor", "section")),
            P(("groups", "tensor", "section"), "split"),
        ),
        check_vma=False,
    )
```

```python
import jax
import jax.numpy as jnp
from jax import lax
from jax.experimental import pallas as pl
from jax.experimental.pallas import tpu as pltpu
from jax.sharding import PartitionSpec as P


def bit_count(size):
    return size.bit_length() - 1


def phase_orders():
    section = [("section", b) for b in range(bit_count(lax.axis_size("section")))]
    tensor = [("tensor", b) for b in range(bit_count(lax.axis_size("tensor")))]
    return section + tensor, tensor[:1] + section + tensor[1:]


def phase_swap(value, moves):
    tensors, sections, cores = (lax.axis_size(a) for a in ("tensor", "section", "split"))
    pairs = []
    for t in range(tensors):
        for s in range(sections):
            for c in range(cores):
                axis, bit = moves[c]
                to_t = t ^ (1 << bit) if axis == "tensor" else t
                to_s = s ^ (1 << bit) if axis == "section" else s
                pairs.append(((t * sections + s) * cores + c, (to_t * sections + to_s) * cores + c))
    return lax.ppermute(value, ("tensor", "section", "split"), pairs)


def swapped(value, axis, bit):
    pairs = [(source, source ^ (1 << bit)) for source in range(lax.axis_size(axis))]
    return lax.ppermute(value, axis, pairs)


def general(
    teacher_hidden,
    teacher_gain,
    proj_weight,
    student_input,
    student_gain,
    gate_weight,
    up_weight,
    down_weight,
    block_order,
):
    eps = 1e-05
    bf16, f32 = jnp.bfloat16, jnp.float32
    tensors, sections = lax.axis_size("tensor"), lax.axis_size("section")
    core = lax.axis_index("split")
    orders = phase_orders()
    phases = list(zip(*orders))
    index = {"tensor": lax.axis_index("tensor"), "section": lax.axis_index("section")}

    def bit_of(axis, bit):
        return (index[axis] >> bit) & 1

    bits = [jnp.where(core == 0, bit_of(*a), bit_of(*b)) for a, b in phases]
    count = len(phases)

    def owned(which):
        return sum(bit_of(*axis_bit) << (count - 1 - k) for k, axis_bit in enumerate(orders[which]))

    def gathered(value):
        for k in reversed(range(count)):
            got = phase_swap(value, phases[k])
            value = jnp.where(
                bits[k] == 1,
                jnp.concatenate([got, value], axis=1),
                jnp.concatenate([value, got], axis=1),
            )
        return value

    def natural(value):
        rows, cols = value.shape
        blocks = value.reshape((rows,) + (2,) * count + (cols >> count,))
        wanted = [("tensor", b) for b in reversed(range(bit_count(tensors)))]
        wanted += [("section", b) for b in reversed(range(bit_count(sections)))]
        forms = []
        for order in orders:
            axes = [0] + [1 + order.index(w) for w in wanted] + [1 + count]
            forms.append(jnp.transpose(blocks, axes).reshape(rows, cols))
        return jnp.where(core == 0, forms[0], forms[1])

    whole_input = natural(gathered(student_input))
    whole_gain = natural(gathered(student_gain[None, :]))[0]
    own_rows, width = whole_input.shape
    half_width = width // 2

    teach_local = teacher_hidden.astype(f32)
    total_sq = jnp.sum(teach_local * teach_local, axis=1)
    for b in range(bit_count(tensors)):
        total_sq = total_sq + swapped(total_sq, "tensor", b)
    narrow = teacher_hidden.shape[1] // sections
    section = index["section"]
    if sections == 2:
        away = lax.dynamic_slice_in_dim(teacher_hidden, (1 - section) * narrow, narrow, 1)
        stay = lax.dynamic_slice_in_dim(teacher_hidden, section * narrow, narrow, 1)
        moved = jnp.concatenate([stay, swapped(away, "section", 0)], axis=0)
        total_sq = jnp.concatenate([total_sq, swapped(total_sq, "section", 0)])
        block = teacher_hidden.shape[0]
        picks = block_order ^ (section * block) if block & (block - 1) == 0 else (
            (block_order // block) ^ section
        ) * block + block_order % block
    else:
        moved = lax.all_to_all(teacher_hidden, "section", split_axis=1, concat_axis=0, tiled=True)
        total_sq = lax.all_gather(total_sq, "section", axis=0, tiled=True)
        picks = block_order
    piece_gain = lax.dynamic_slice_in_dim(teacher_gain, section * narrow, narrow, 0)
    teacher_width = narrow * tensors * sections
    scaled = moved.astype(f32) * lax.rsqrt(total_sq / teacher_width + eps)[:, None] * piece_gain
    teacher_normed = scaled.astype(bf16)
    chosen = (picks[:, None] == jnp.arange(own_rows)[None, :]).astype(bf16)
    arranged = jnp.dot(chosen, teacher_normed, preferred_element_type=f32).astype(bf16)
    arranged_pair = jnp.concatenate([arranged, swapped(arranged, "split", 0)], axis=0)
    target = jnp.dot(arranged_pair, proj_weight, preferred_element_type=f32)

    inputs = whole_input.astype(f32)
    stu_sq = jnp.mean(inputs * inputs, axis=1, keepdims=True)
    normed = (inputs * lax.rsqrt(stu_sq + eps) * whole_gain.astype(f32)).astype(bf16)
    normed_away = lax.dynamic_slice_in_dim(normed, (1 - core) * half_width, half_width, 1)
    normed_stay = lax.dynamic_slice_in_dim(normed, core * half_width, half_width, 1)
    normed_pair = jnp.concatenate([normed_stay, swapped(normed_away, "split", 0)], axis=0)
    part_cols = half_width >> count
    mine = jnp.where(core == 0, owned(0), owned(1))
    other = jnp.where(core == 0, owned(1), owned(0))
    input_stay = lax.dynamic_slice_in_dim(
        whole_input, core * half_width + mine * part_cols, part_cols, 1
    )
    input_away = lax.dynamic_slice_in_dim(
        whole_input, (1 - core) * half_width + other * part_cols, part_cols, 1
    )
    input_pair = jnp.concatenate([input_stay, swapped(input_away, "split", 0)], axis=0)
    gate = jnp.dot(normed, gate_weight, preferred_element_type=f32)
    up = jnp.dot(normed, up_weight, preferred_element_type=f32)
    active = jax.nn.silu(gate)
    hidden = (active * up).astype(bf16)
    hidden_pair = jnp.concatenate([hidden, swapped(hidden, "split", 0)], axis=0)

    down_half = lax.dynamic_slice_in_dim(down_weight, core * half_width, half_width, 1)
    current = jnp.dot(hidden_pair, down_half, preferred_element_type=f32) - target
    for k in range(count):
        half = current.shape[1] // 2
        away = lax.dynamic_slice_in_dim(current, (1 - bits[k]) * half, half, 1).astype(bf16)
        stay = lax.dynamic_slice_in_dim(current, bits[k] * half, half, 1)
        current = stay + phase_swap(away, phases[k]).astype(f32)
    total_rows = own_rows * lax.axis_size("split")
    difference = input_pair.astype(f32) + current
    cotangent_half = gathered((difference * (64.0 / total_rows)).astype(bf16))

    cot_stay, cot_away = cotangent_half[:own_rows], cotangent_half[own_rows:]
    cot_got = swapped(cot_away, "split", 0)
    cotangent = jnp.where(
        core == 0,
        jnp.concatenate([cot_stay, cot_got], axis=1),
        jnp.concatenate([cot_got, cot_stay], axis=1),
    )
    back_hidden = lax.dot_general(
        cotangent, down_weight, (((1,), (1,)), ((), ())), preferred_element_type=f32
    )
    sigma = jax.nn.sigmoid(gate)
    d_gate = (back_hidden * up * sigma * (1.0 + gate * (1.0 - sigma))).astype(bf16)
    d_up = (back_hidden * active).astype(bf16)
    got_gate, got_up = swapped((d_gate, d_up), "split", 0)
    d_gate_pair = jnp.concatenate([d_gate, got_gate], axis=0)
    d_up_pair = jnp.concatenate([d_up, got_up], axis=0)
    contract_rows = (((0,), (0,)), ((), ()))

    def over_rows(left, right):
        return lax.dot_general(left, right, contract_rows, preferred_element_type=f32).astype(bf16)

    grad_down = over_rows(hidden_pair, cotangent_half)
    grad_gate = over_rows(normed_pair, d_gate_pair)
    grad_up = over_rows(normed_pair, d_up_pair)
    return grad_gate, grad_up, grad_down


TILE = 256
GAIN_ROWS = 16
LIMIT = 56 * 1024 * 1024


def kernel_params():
    return pltpu.CompilerParams(vmem_limit_bytes=LIMIT)


def whole(shape):
    return pl.BlockSpec(shape, lambda *_: (0,) * len(shape))


def normalise(pieces, info, eps, width):
    rows, cols = pieces[0].shape[0] - GAIN_ROWS, pieces[0].shape[1]
    count = len(pieces)
    step = 64

    def body(info_ref, *refs):
        blocks, (stay, away, raw_stay, raw_away) = refs[:count], refs[count:]
        core, want_stay, want_away = info_ref[count], info_ref[count + 1], info_ref[count + 2]
        per_half = count // 2

        def chunk(i, _):
            at = pl.multiple_of(i * step, step)
            partial = jnp.zeros((step, 128), jnp.float32)
            for block in blocks:
                value = block[pl.ds(at, step), :].astype(jnp.float32)
                square = value * value
                for k in range(cols // 128):
                    partial = partial + square[:, k * 128 : (k + 1) * 128]
            total = jnp.sum(partial, axis=1, keepdims=True)
            scale = lax.rsqrt(total / width + eps)
            for j, block in enumerate(blocks):
                place = info_ref[j]
                inside = place % per_half
                gain = block[rows : rows + 1, :].astype(jnp.float32)
                value = block[pl.ds(at, step), :]
                scaled = (value.astype(jnp.float32) * scale * gain).astype(jnp.bfloat16)
                where = pl.ds(pl.multiple_of(inside * cols, cols), cols)

                @pl.when(place // per_half == core)
                def _():
                    stay[pl.ds(at, step), where] = scaled

                @pl.when(place // per_half != core)
                def _():
                    away[pl.ds(at, step), where] = scaled

                @pl.when(place == want_stay)
                def _():
                    raw_stay[pl.ds(at, step), :] = value

                @pl.when(place == want_away)
                def _():
                    raw_away[pl.ds(at, step), :] = value

            return 0

        lax.fori_loop(0, rows // step, chunk, 0)

    half = jax.ShapeDtypeStruct((rows, cols * count // 2), jnp.bfloat16)
    raw = jax.ShapeDtypeStruct((rows, cols), jnp.bfloat16)
    return pl.pallas_call(
        body,
        out_shape=(half, half, raw, raw),
        grid_spec=pltpu.PrefetchScalarGridSpec(
            num_scalar_prefetch=1,
            grid=(1,),
            in_specs=[whole(p.shape) for p in pieces],
            out_specs=[whole(half.shape), whole(half.shape), whole(raw.shape), whole(raw.shape)],
        ),
        compiler_params=kernel_params(),
        name="normalise",
    )(info, *pieces)


def forward(stay, away, gate_weight, up_weight, core):
    rows, half = stay.shape
    hidden_units = gate_weight.shape[1]

    def body(core_ref, stay_ref, away_ref, gs, ga, us, ua, hidden_ref, gate_ref, up_ref):
        def product(near, far):
            return jnp.dot(stay_ref[...], near[...], preferred_element_type=jnp.float32) + jnp.dot(
                away_ref[...], far[...], preferred_element_type=jnp.float32
            )

        gate = product(gs, ga)
        up = product(us, ua)
        gate_ref[...] = gate
        up_ref[...] = up
        hidden_ref[...] = (gate / (1.0 + jnp.exp(-gate)) * up).astype(jnp.bfloat16)

    near = pl.BlockSpec((half, TILE), lambda i, core: (core[0], i))
    far = pl.BlockSpec((half, TILE), lambda i, core: (1 - core[0], i))
    tile = pl.BlockSpec((rows, TILE), lambda i, core: (0, i))
    return pl.pallas_call(
        body,
        out_shape=(
            jax.ShapeDtypeStruct((rows, hidden_units), jnp.bfloat16),
            jax.ShapeDtypeStruct((rows, hidden_units), jnp.float32),
            jax.ShapeDtypeStruct((rows, hidden_units), jnp.float32),
        ),
        grid_spec=pltpu.PrefetchScalarGridSpec(
            num_scalar_prefetch=1,
            grid=(hidden_units // TILE,),
            in_specs=[whole(stay.shape), whole(away.shape), near, far, near, far],
            out_specs=[tile, tile, tile],
        ),
        compiler_params=kernel_params(),
        name="forward",
    )(core, stay, away, gate_weight, gate_weight, up_weight, up_weight)


def project_down(hidden, down_weight, target, info):
    rows, hidden_units = hidden.shape
    half = target.shape[1]
    tiles = half // TILE
    mid = tiles // 2

    def place(i, info):
        return jnp.where(i < mid, (1 - info[1]) * mid + i, info[1] * mid + i - mid)

    def body(info_ref, hidden_ref, down_ref, target_ref, send_ref, keep_ref):
        value = (
            jnp.dot(hidden_ref[...], down_ref[...], preferred_element_type=jnp.float32)
            - target_ref[...]
        )

        @pl.when(pl.program_id(0) < mid)
        def _():
            send_ref[...] = value.astype(jnp.bfloat16)

        @pl.when(pl.program_id(0) >= mid)
        def _():
            keep_ref[...] = value

    return pl.pallas_call(
        body,
        out_shape=(
            jax.ShapeDtypeStruct((rows, half // 2), jnp.bfloat16),
            jax.ShapeDtypeStruct((rows, half // 2), jnp.float32),
        ),
        grid_spec=pltpu.PrefetchScalarGridSpec(
            num_scalar_prefetch=1,
            grid=(tiles,),
            in_specs=[
                whole(hidden.shape),
                pl.BlockSpec((hidden_units, TILE), lambda i, info: (0, info[0] * tiles + place(i, info))),
                pl.BlockSpec((rows, TILE), lambda i, info: (0, place(i, info))),
            ],
            out_specs=[
                pl.BlockSpec((rows, TILE), lambda i, info: (0, jnp.minimum(i, mid - 1))),
                pl.BlockSpec((rows, TILE), lambda i, info: (0, jnp.maximum(i - mid, 0))),
            ],
        ),
        compiler_params=kernel_params(),
        name="project_down",
    )(info, hidden, down_weight, target)


def backward(cots, places, down_weight, gate, up):
    rows, cols = cots[0].shape
    hidden_units, width = down_weight.shape
    count = len(cots)

    def body(places_ref, *refs):
        blocks, (down_ref, gate_ref, up_ref, d_gate_ref, d_up_ref) = refs[:count], refs[count:]
        back = jnp.zeros((rows, TILE), jnp.float32)
        for j, block in enumerate(blocks):
            at = pl.ds(pl.multiple_of(places_ref[j] * cols, cols), cols)
            back = back + lax.dot_general(
                block[...], down_ref[:, at], (((1,), (1,)), ((), ())),
                preferred_element_type=jnp.float32,
            )
        gate, up = gate_ref[...], up_ref[...]
        sigma = 1.0 / (1.0 + jnp.exp(-gate))
        d_gate_ref[...] = (back * up * sigma * (1.0 + gate * (1.0 - sigma))).astype(jnp.bfloat16)
        d_up_ref[...] = (back * (gate * sigma)).astype(jnp.bfloat16)

    tile = pl.BlockSpec((rows, TILE), lambda i, places: (0, i))
    out = jax.ShapeDtypeStruct((rows, hidden_units), jnp.bfloat16)
    return pl.pallas_call(
        body,
        out_shape=(out, out),
        grid_spec=pltpu.PrefetchScalarGridSpec(
            num_scalar_prefetch=1,
            grid=(hidden_units // TILE,),
            in_specs=[whole(c.shape) for c in cots]
            + [pl.BlockSpec((TILE, width), lambda i, places: (i, 0)), tile, tile],
            out_specs=[tile, tile],
        ),
        compiler_params=kernel_params(),
        name="backward",
    )(places, *cots, down_weight, gate, up)


def down_gradient(left_own, left_other, own, other, places):
    hidden_units, rows = left_own.shape
    cols = own[0].shape[1]
    count = len(own)

    def body(places_ref, lo, lt, *refs):
        near, far, out = refs[:count], refs[count : 2 * count], refs[2 * count]
        for j in range(count):
            at = pl.ds(pl.multiple_of(places_ref[j] * cols, cols), cols)
            out[:, at] = (
                jnp.dot(lo[...], near[j][...], preferred_element_type=jnp.float32)
                + jnp.dot(lt[...], far[j][...], preferred_element_type=jnp.float32)
            ).astype(jnp.bfloat16)

    tile = pl.BlockSpec((TILE, rows), lambda i, places: (i, 0))
    return pl.pallas_call(
        body,
        out_shape=jax.ShapeDtypeStruct((hidden_units, cols * count), jnp.bfloat16),
        grid_spec=pltpu.PrefetchScalarGridSpec(
            num_scalar_prefetch=1,
            grid=(hidden_units // TILE,),
            in_specs=[tile, tile] + [whole(p.shape) for p in (*own, *other)],
            out_specs=pl.BlockSpec((TILE, cols * count), lambda i, places: (i, 0)),
        ),
        compiler_params=kernel_params(),
        name="down_gradient",
    )(places, left_own, left_other, *own, *other)


def input_gradients(left_own, left_other, gate_own, gate_other, up_own, up_other):
    width, rows = left_own.shape
    hidden_units = gate_own.shape[1]

    def body(lo, lt, go, gt, uo, ut, gate_ref, up_ref):
        for own, other, out in ((go, gt, gate_ref), (uo, ut, up_ref)):
            out[...] = (
                jnp.dot(lo[...], own[...], preferred_element_type=jnp.float32)
                + jnp.dot(lt[...], other[...], preferred_element_type=jnp.float32)
            ).astype(jnp.bfloat16)

    tile = pl.BlockSpec((rows, TILE), lambda i: (0, i))
    out = jax.ShapeDtypeStruct((width, hidden_units), jnp.bfloat16)
    return pl.pallas_call(
        body,
        out_shape=(out, out),
        grid=(hidden_units // TILE,),
        in_specs=[whole(left_own.shape), whole(left_other.shape), tile, tile, tile, tile],
        out_specs=[pl.BlockSpec((width, TILE), lambda i: (0, i))] * 2,
        compiler_params=kernel_params(),
        name="input_gradients",
    )(left_own, left_other, gate_own, gate_other, up_own, up_other)


def tiled(
    teacher_hidden,
    teacher_gain,
    proj_weight,
    student_input,
    student_gain,
    gate_weight,
    up_weight,
    down_weight,
    block_order,
):
    eps = 1e-05
    bf16, f32 = jnp.bfloat16, jnp.float32
    core, section, tensor = (lax.axis_index(a) for a in ("split", "section", "tensor"))
    low, high = tensor & 1, tensor >> 1
    first = (("section", 0), ("tensor", 0))
    second = (("tensor", 0), ("section", 0))
    across = (("tensor", 1), ("tensor", 1))
    bit1 = jnp.where(core == 0, section, low)
    bit2 = jnp.where(core == 0, low, section)
    mask1 = jnp.where(core == 0, 1, 2)
    mask2 = 3 - mask1

    def partner(value):
        return swapped(value, "split", 0)

    rows, cols = student_input.shape
    own = jnp.concatenate(
        [student_input, jnp.broadcast_to(student_gain[None, :], (GAIN_ROWS, cols))], axis=0
    )
    far = phase_swap(own, across)
    near2 = phase_swap(own, second)
    near1 = phase_swap(own, first)
    near12 = phase_swap(near2, first)
    far2 = phase_swap(far, second)
    far1 = phase_swap(far, first)
    far12 = phase_swap(far2, first)
    me = tensor * 2 + section
    masks = (0, 4, mask2, mask1, 3, 4 ^ mask2, 4 ^ mask1, 7)
    block_own = bit1 * 2 + bit2
    block_other = bit2 * 2 + bit1
    info = jnp.stack(
        [me ^ m for m in masks] + [core, core * 4 + block_own, (1 - core) * 4 + block_other]
    ).astype(jnp.int32)
    width = cols * 8
    normed, normed_away, raw, raw_away = normalise(
        (own, far, near2, near1, near12, far2, far1, far12), info, eps, width
    )

    teach_local = teacher_hidden.astype(f32)
    total_sq = jnp.sum(teach_local * teach_local, axis=1)
    total_sq = total_sq + swapped(total_sq, "tensor", 0)
    total_sq = total_sq + swapped(total_sq, "tensor", 1)
    total_sq = jnp.concatenate([total_sq, swapped(total_sq, "section", 0)])
    block, narrow = teacher_hidden.shape[0], teacher_hidden.shape[1] // 2
    leave = lax.dynamic_slice_in_dim(teacher_hidden, (1 - section) * narrow, narrow, 1)
    remain = lax.dynamic_slice_in_dim(teacher_hidden, section * narrow, narrow, 1)
    moved = jnp.concatenate([remain, swapped(leave, "section", 0)], axis=0)
    picks = ((block_order // block) ^ section) * block + block_order % block
    piece_gain = lax.dynamic_slice_in_dim(teacher_gain, section * narrow, narrow, 0)
    scaled = moved.astype(f32) * lax.rsqrt(total_sq / (narrow * 8) + eps)[:, None] * piece_gain
    chosen = (picks[:, None] == jnp.arange(rows)[None, :]).astype(bf16)
    arranged = jnp.dot(chosen, scaled.astype(bf16), preferred_element_type=f32).astype(bf16)
    target_own = jnp.dot(arranged, proj_weight, preferred_element_type=f32)
    target_other = jnp.dot(partner(arranged), proj_weight, preferred_element_type=f32)

    core_info = core[None].astype(jnp.int32)
    hidden, gate, up = forward(normed, normed_away, gate_weight, up_weight, core_info)
    normed_other = partner(normed_away)
    raw_other = partner(raw_away)
    hidden_other = partner(hidden)

    down_info = jnp.stack([core, bit1]).astype(jnp.int32)
    scale = 64.0 / (rows * 2)

    def cotangent_of(hidden_rows, target, input_block):
        send, keep = project_down(hidden_rows, down_weight, target, down_info)
        current = keep + phase_swap(send, first).astype(f32)
        half = current.shape[1] // 2
        send = lax.dynamic_slice_in_dim(current, (1 - bit2) * half, half, 1).astype(bf16)
        keep = lax.dynamic_slice_in_dim(current, bit2 * half, half, 1)
        current = keep + phase_swap(send, second).astype(f32)
        current = current + phase_swap(current.astype(bf16), across).astype(f32)
        piece = ((input_block.astype(f32) + current) * scale).astype(bf16)
        piece2 = phase_swap(piece, second)
        piece1 = phase_swap(piece, first)
        return piece, piece2, piece1, phase_swap(piece2, first)

    cots_own = cotangent_of(hidden, target_own, raw)
    cots_other = cotangent_of(hidden_other, target_other, raw_other)
    cots_got = tuple(partner(p) for p in cots_other)

    order = (0, 1, 2, 3)
    places_own = [block_own ^ m for m in order]
    places_got = [block_other ^ m for m in order]
    places = jnp.stack(
        [core * 4 + p for p in places_own] + [(1 - core) * 4 + p for p in places_got]
    ).astype(jnp.int32)
    d_gate, d_up = backward((*cots_own, *cots_got), places, down_weight, gate, up)
    d_gate_other, d_up_other = partner(d_gate), partner(d_up)
    grad_down = down_gradient(
        hidden.T, hidden_other.T, cots_own, cots_other, jnp.stack(places_own).astype(jnp.int32)
    )
    grad_gate, grad_up = input_gradients(
        normed.T, normed_other.T, d_gate, d_gate_other, d_up, d_up_other
    )
    return grad_gate, grad_up, grad_down


def fits_tiles(teacher_hidden, proj_weight, student_input, gate_weight):
    axes = tuple(lax.axis_size(a) for a in ("tensor", "section", "split"))
    rows, cols = student_input.shape
    return (
        axes == (4, 2, 2)
        and cols % TILE == 0
        and rows % TILE == 0
        and gate_weight.shape[1] % TILE == 0
        and proj_weight.shape[1] % (2 * TILE) == 0
        and teacher_hidden.shape[0] * 2 == rows
        and teacher_hidden.shape[1] % TILE == 0
    )


def on_device(*arrays):
    teacher_hidden, _, proj_weight, student_input, _, gate_weight = arrays[:6]
    plan = tiled if fits_tiles(teacher_hidden, proj_weight, student_input, gate_weight) else general
    return plan(*arrays)


def solution(mesh):
    placed = (
        P(("groups", "section", "split"), "tensor"),
        P("tensor"),
        P(("tensor", "section"), "split"),
        P(("groups", "split"), ("tensor", "section")),
        P(("tensor", "section")),
        P(None, ("tensor", "section")),
        P(None, ("tensor", "section")),
        P(("tensor", "section"), None),
        P(),
    )
    return jax.shard_map(
        on_device,
        mesh=mesh,
        in_specs=placed,
        out_specs=(
            P(("groups", "split"), ("tensor", "section")),
            P(("groups", "split"), ("tensor", "section")),
            P(("groups", "tensor", "section"), "split"),
        ),
        check_vma=False,
    )
```

```python
import jax
import jax.numpy as jnp
from jax import lax
from jax.experimental import pallas as pl
from jax.experimental.pallas import tpu as pltpu
from jax.sharding import PartitionSpec as P


def bit_count(size):
    return size.bit_length() - 1


def phase_orders():
    section = [("section", b) for b in range(bit_count(lax.axis_size("section")))]
    tensor = [("tensor", b) for b in range(bit_count(lax.axis_size("tensor")))]
    return section + tensor, tensor[:1] + section + tensor[1:]


def phase_swap(value, moves):
    tensors, sections, cores = (lax.axis_size(a) for a in ("tensor", "section", "split"))
    pairs = []
    for t in range(tensors):
        for s in range(sections):
            for c in range(cores):
                axis, bit = moves[c]
                to_t = t ^ (1 << bit) if axis == "tensor" else t
                to_s = s ^ (1 << bit) if axis == "section" else s
                pairs.append(((t * sections + s) * cores + c, (to_t * sections + to_s) * cores + c))
    return lax.ppermute(value, ("tensor", "section", "split"), pairs)


def swapped(value, axis, bit):
    pairs = [(source, source ^ (1 << bit)) for source in range(lax.axis_size(axis))]
    return lax.ppermute(value, axis, pairs)


def general(
    teacher_hidden,
    teacher_gain,
    proj_weight,
    student_input,
    student_gain,
    gate_weight,
    up_weight,
    down_weight,
    block_order,
):
    eps = 1e-05
    bf16, f32 = jnp.bfloat16, jnp.float32
    tensors, sections = lax.axis_size("tensor"), lax.axis_size("section")
    core = lax.axis_index("split")
    orders = phase_orders()
    phases = list(zip(*orders))
    index = {"tensor": lax.axis_index("tensor"), "section": lax.axis_index("section")}

    def bit_of(axis, bit):
        return (index[axis] >> bit) & 1

    bits = [jnp.where(core == 0, bit_of(*a), bit_of(*b)) for a, b in phases]
    count = len(phases)

    def owned(which):
        return sum(bit_of(*axis_bit) << (count - 1 - k) for k, axis_bit in enumerate(orders[which]))

    def gathered(value):
        for k in reversed(range(count)):
            got = phase_swap(value, phases[k])
            value = jnp.where(
                bits[k] == 1,
                jnp.concatenate([got, value], axis=1),
                jnp.concatenate([value, got], axis=1),
            )
        return value

    def natural(value):
        rows, cols = value.shape
        blocks = value.reshape((rows,) + (2,) * count + (cols >> count,))
        wanted = [("tensor", b) for b in reversed(range(bit_count(tensors)))]
        wanted += [("section", b) for b in reversed(range(bit_count(sections)))]
        forms = []
        for order in orders:
            axes = [0] + [1 + order.index(w) for w in wanted] + [1 + count]
            forms.append(jnp.transpose(blocks, axes).reshape(rows, cols))
        return jnp.where(core == 0, forms[0], forms[1])

    whole_input = natural(gathered(student_input))
    whole_gain = natural(gathered(student_gain[None, :]))[0]
    own_rows, width = whole_input.shape
    half_width = width // 2

    teach_local = teacher_hidden.astype(f32)
    total_sq = jnp.sum(teach_local * teach_local, axis=1)
    for b in range(bit_count(tensors)):
        total_sq = total_sq + swapped(total_sq, "tensor", b)
    narrow = teacher_hidden.shape[1] // sections
    section = index["section"]
    if sections == 2:
        away = lax.dynamic_slice_in_dim(teacher_hidden, (1 - section) * narrow, narrow, 1)
        stay = lax.dynamic_slice_in_dim(teacher_hidden, section * narrow, narrow, 1)
        moved = jnp.concatenate([stay, swapped(away, "section", 0)], axis=0)
        total_sq = jnp.concatenate([total_sq, swapped(total_sq, "section", 0)])
        block = teacher_hidden.shape[0]
        picks = block_order ^ (section * block) if block & (block - 1) == 0 else (
            (block_order // block) ^ section
        ) * block + block_order % block
    else:
        moved = lax.all_to_all(teacher_hidden, "section", split_axis=1, concat_axis=0, tiled=True)
        total_sq = lax.all_gather(total_sq, "section", axis=0, tiled=True)
        picks = block_order
    piece_gain = lax.dynamic_slice_in_dim(teacher_gain, section * narrow, narrow, 0)
    teacher_width = narrow * tensors * sections
    scaled = moved.astype(f32) * lax.rsqrt(total_sq / teacher_width + eps)[:, None] * piece_gain
    teacher_normed = scaled.astype(bf16)
    chosen = (picks[:, None] == jnp.arange(own_rows)[None, :]).astype(bf16)
    arranged = jnp.dot(chosen, teacher_normed, preferred_element_type=f32).astype(bf16)
    arranged_pair = jnp.concatenate([arranged, swapped(arranged, "split", 0)], axis=0)
    target = jnp.dot(arranged_pair, proj_weight, preferred_element_type=f32)

    inputs = whole_input.astype(f32)
    stu_sq = jnp.mean(inputs * inputs, axis=1, keepdims=True)
    normed = (inputs * lax.rsqrt(stu_sq + eps) * whole_gain.astype(f32)).astype(bf16)
    normed_away = lax.dynamic_slice_in_dim(normed, (1 - core) * half_width, half_width, 1)
    normed_stay = lax.dynamic_slice_in_dim(normed, core * half_width, half_width, 1)
    normed_pair = jnp.concatenate([normed_stay, swapped(normed_away, "split", 0)], axis=0)
    part_cols = half_width >> count
    mine = jnp.where(core == 0, owned(0), owned(1))
    other = jnp.where(core == 0, owned(1), owned(0))
    input_stay = lax.dynamic_slice_in_dim(
        whole_input, core * half_width + mine * part_cols, part_cols, 1
    )
    input_away = lax.dynamic_slice_in_dim(
        whole_input, (1 - core) * half_width + other * part_cols, part_cols, 1
    )
    input_pair = jnp.concatenate([input_stay, swapped(input_away, "split", 0)], axis=0)
    gate = jnp.dot(normed, gate_weight, preferred_element_type=f32)
    up = jnp.dot(normed, up_weight, preferred_element_type=f32)
    active = jax.nn.silu(gate)
    hidden = (active * up).astype(bf16)
    hidden_pair = jnp.concatenate([hidden, swapped(hidden, "split", 0)], axis=0)

    down_half = lax.dynamic_slice_in_dim(down_weight, core * half_width, half_width, 1)
    current = jnp.dot(hidden_pair, down_half, preferred_element_type=f32) - target
    for k in range(count):
        half = current.shape[1] // 2
        away = lax.dynamic_slice_in_dim(current, (1 - bits[k]) * half, half, 1).astype(bf16)
        stay = lax.dynamic_slice_in_dim(current, bits[k] * half, half, 1)
        current = stay + phase_swap(away, phases[k]).astype(f32)
    total_rows = own_rows * lax.axis_size("split")
    difference = input_pair.astype(f32) + current
    cotangent_half = gathered((difference * (64.0 / total_rows)).astype(bf16))

    cot_stay, cot_away = cotangent_half[:own_rows], cotangent_half[own_rows:]
    cot_got = swapped(cot_away, "split", 0)
    cotangent = jnp.where(
        core == 0,
        jnp.concatenate([cot_stay, cot_got], axis=1),
        jnp.concatenate([cot_got, cot_stay], axis=1),
    )
    back_hidden = lax.dot_general(
        cotangent, down_weight, (((1,), (1,)), ((), ())), preferred_element_type=f32
    )
    sigma = jax.nn.sigmoid(gate)
    d_gate = (back_hidden * up * sigma * (1.0 + gate * (1.0 - sigma))).astype(bf16)
    d_up = (back_hidden * active).astype(bf16)
    got_gate, got_up = swapped((d_gate, d_up), "split", 0)
    d_gate_pair = jnp.concatenate([d_gate, got_gate], axis=0)
    d_up_pair = jnp.concatenate([d_up, got_up], axis=0)
    contract_rows = (((0,), (0,)), ((), ()))

    def over_rows(left, right):
        return lax.dot_general(left, right, contract_rows, preferred_element_type=f32).astype(bf16)

    grad_down = over_rows(hidden_pair, cotangent_half)
    grad_gate = over_rows(normed_pair, d_gate_pair)
    grad_up = over_rows(normed_pair, d_up_pair)
    return grad_gate, grad_up, grad_down


TILE = 256
GAIN_ROWS = 16
MIB = 1024 * 1024


def run_kernel(body, inputs, outputs, scratch, name, limit):
    return pl.pallas_call(
        body,
        out_shape=outputs,
        in_specs=[pl.BlockSpec(memory_space=pltpu.SMEM)]
        + [pl.BlockSpec(memory_space=pl.ANY)] * (len(inputs) - 1),
        out_specs=[
            pl.BlockSpec(memory_space=pl.ANY if out.shape[0] > 1024 else pltpu.VMEM) for out in outputs
        ],
        scratch_shapes=scratch,
        compiler_params=pltpu.CompilerParams(vmem_limit_bytes=limit * MIB),
        name=name,
    )(*inputs)


def aligned(index, size):
    return pl.ds(pl.multiple_of(index * size, size), size)


def forward(pieces, gate_weight, up_weight, info, eps, width):
    rows, cols = pieces[0].shape[0] - GAIN_ROWS, pieces[0].shape[1]
    count = len(pieces)
    per_half = count // 2
    hidden_units = gate_weight.shape[1]
    step = 64

    def body(info_ref, *refs):
        sources, (gate_hbm, up_hbm) = refs[:count], refs[count : count + 2]
        stay, away, raw_stay, raw_away, hidden_ref, gate_ref, up_ref = refs[count + 2 : count + 9]
        blocks, ready, gates, ups, block_sem, gate_sem, up_sem = refs[count + 9 :]
        core, want_stay, want_away = info_ref[count], info_ref[count + 1], info_ref[count + 2]

        def block_copy(j):
            return pltpu.make_async_copy(sources[j], blocks.at[j], block_sem.at[j])

        def gate_copy(j):
            return pltpu.make_async_copy(
                gate_hbm.at[aligned(info_ref[j], cols), :], gates.at[j], gate_sem.at[j]
            )

        def up_copy(j):
            return pltpu.make_async_copy(
                up_hbm.at[aligned(info_ref[j], cols), :], ups.at[j], up_sem.at[j]
            )

        for j in range(count):
            block_copy(j).start()
        for j in range(count):
            gate_copy(j).start()
            up_copy(j).start()
        for j in range(count):
            block_copy(j).wait()

        def chunk(i, _):
            at = aligned(i, step)

            def square(j, partial):
                value = blocks[j, at, :].astype(jnp.float32)
                value = value * value
                for k in range(cols // 128):
                    partial = partial + value[:, k * 128 : (k + 1) * 128]
                return partial

            partial = lax.fori_loop(0, count, square, jnp.zeros((step, 128), jnp.float32))
            scale = lax.rsqrt(jnp.sum(partial, axis=1, keepdims=True) / width + eps)

            def norm(j, _):
                place = info_ref[j]
                where = aligned(place % per_half, cols)
                gain = blocks[j, rows : rows + 1, :].astype(jnp.float32)
                value = blocks[j, at, :]
                scaled = (value.astype(jnp.float32) * scale * gain).astype(jnp.bfloat16)
                ready[j, at, :] = scaled

                @pl.when(place // per_half == core)
                def _():
                    stay[at, where] = scaled

                @pl.when(place // per_half != core)
                def _():
                    away[at, where] = scaled

                @pl.when(place == want_stay)
                def _():
                    raw_stay[at, :] = value

                @pl.when(place == want_away)
                def _():
                    raw_away[at, :] = value

                return 0

            return lax.fori_loop(0, count, norm, 0)

        lax.fori_loop(0, rows // step, chunk, 0)

        def product(j):
            gate_copy(j).wait()
            near = jnp.dot(ready[j], gates[j], preferred_element_type=jnp.float32)
            up_copy(j).wait()
            return near, jnp.dot(ready[j], ups[j], preferred_element_type=jnp.float32)

        gate_ref[...] = jnp.zeros_like(gate_ref)
        up_ref[...] = jnp.zeros_like(up_ref)

        def accumulate(j, _):
            near, far = product(j)
            gate_ref[...] += near
            up_ref[...] += far
            return 0

        lax.fori_loop(0, count, accumulate, 0)

        def finish(i, _):
            at = aligned(i, 32)
            gate = gate_ref[at, :]
            hidden_ref[at, :] = (gate / (1.0 + jnp.exp(-gate)) * up_ref[at, :]).astype(jnp.bfloat16)
            return 0

        lax.fori_loop(0, rows // 32, finish, 0)

    half = jax.ShapeDtypeStruct((rows, cols * per_half), jnp.bfloat16)
    raw = jax.ShapeDtypeStruct((rows, cols), jnp.bfloat16)
    wide = jax.ShapeDtypeStruct((rows, hidden_units), jnp.float32)
    outputs = (half, half, raw, raw, jax.ShapeDtypeStruct(wide.shape, jnp.bfloat16), wide, wide)
    weights = pltpu.VMEM((count, cols, hidden_units), jnp.bfloat16)
    sems = pltpu.SemaphoreType.DMA((count,))
    scratch = [
        pltpu.VMEM((count,) + pieces[0].shape, jnp.bfloat16),
        pltpu.VMEM((count, rows, cols), jnp.bfloat16),
        weights,
        weights,
        sems,
        sems,
        sems,
    ]
    return run_kernel(body, (info, *pieces, gate_weight, up_weight), outputs, scratch, "forward", 52)


def project_down(hidden, down_weight, target, scale, info):
    rows, hidden_units = hidden.shape
    half = target.shape[1]
    part = half // 4

    def body(info_ref, hidden_hbm, down_hbm, target_hbm, scale_hbm, send_ref, keep_ref, *scratch):
        left, weights, targets, scales, near_sem, weight_sem, target_sem, scale_sem = scratch
        core, bit = info_ref[0], info_ref[1]
        places = [(1 - bit) * 2, (1 - bit) * 2 + 1, bit * 2, bit * 2 + 1]
        near = pltpu.make_async_copy(hidden_hbm, left, near_sem)
        rate = pltpu.make_async_copy(scale_hbm, scales, scale_sem)
        near.start()
        rate.start()
        loads = []
        for j, place in enumerate(places):
            loads.append(
                (
                    pltpu.make_async_copy(
                        down_hbm.at[:, aligned(core * 4 + place, part)], weights.at[j], weight_sem.at[j]
                    ),
                    pltpu.make_async_copy(
                        target_hbm.at[:, aligned(place, part)], targets.at[j], target_sem.at[j]
                    ),
                )
            )
        for load in loads:
            load[0].start()
            load[1].start()
        near.wait()
        rate.wait()
        for j, load in enumerate(loads):
            load[0].wait()
            load[1].wait()
            value = jnp.dot(left[...], weights[j], preferred_element_type=jnp.float32)
            value = value - targets[j] * scales[:, 0:1]
            at = slice((j % 2) * part, (j % 2 + 1) * part)
            if j < 2:
                send_ref[:, at] = value.astype(jnp.bfloat16)
            else:
                keep_ref[:, at] = value

    outputs = (
        jax.ShapeDtypeStruct((rows, half // 2), jnp.bfloat16),
        jax.ShapeDtypeStruct((rows, half // 2), jnp.float32),
    )
    one, four = pltpu.SemaphoreType.DMA(()), pltpu.SemaphoreType.DMA((4,))
    scratch = [
        pltpu.VMEM((rows, hidden_units), jnp.bfloat16),
        pltpu.VMEM((4, hidden_units, part), jnp.bfloat16),
        pltpu.VMEM((4, rows, part), jnp.float32),
        pltpu.VMEM(scale.shape, jnp.float32),
        one,
        four,
        four,
        one,
    ]
    return run_kernel(
        body, (info, hidden, down_weight, target, scale), outputs, scratch, "project_down", 20
    )


def backward(cots, places, down_weight, gate, up):
    rows, cols = cots[0].shape
    hidden_units, width = down_weight.shape
    count = len(cots)
    steps = hidden_units // TILE

    def body(places_ref, *refs):
        sources, (down_hbm, gate_hbm, up_hbm) = refs[:count], refs[count : count + 3]
        d_gate_ref, d_up_ref = refs[count + 3 : count + 5]
        left, weights, gates, ups, left_sem, weight_sem, gate_sem, up_sem = refs[count + 5 :]

        def weight_copy(i):
            return pltpu.make_async_copy(
                down_hbm.at[aligned(i, TILE), :], weights.at[i], weight_sem.at[i]
            )

        moves = [
            pltpu.make_async_copy(source, left.at[:, aligned(places_ref[j], cols)], left_sem.at[j])
            for j, source in enumerate(sources)
        ]
        for move in moves:
            move.start()
        sides = (
            pltpu.make_async_copy(gate_hbm, gates, gate_sem),
            pltpu.make_async_copy(up_hbm, ups, up_sem),
        )
        weight_copy(0).start()
        for side in sides:
            side.start()
        for i in range(1, steps):
            weight_copy(i).start()
        for move in (*moves, *sides):
            move.wait()

        def tile(i, _):
            weight_copy(i).wait()
            back = lax.dot_general(
                left[...], weights[i], (((1,), (1,)), ((), ())), preferred_element_type=jnp.float32
            )
            at = aligned(i, TILE)
            gate = gates[:, at]
            sigma = 1.0 / (1.0 + jnp.exp(-gate))
            d_gate = back * ups[:, at] * sigma * (1.0 + gate * (1.0 - sigma))
            d_gate_ref[:, at] = d_gate.astype(jnp.bfloat16)
            d_up_ref[:, at] = (back * (gate * sigma)).astype(jnp.bfloat16)
            return 0

        lax.fori_loop(0, steps, tile, 0)

    out = jax.ShapeDtypeStruct((rows, hidden_units), jnp.bfloat16)
    one = pltpu.SemaphoreType.DMA(())
    scratch = [
        pltpu.VMEM((rows, width), jnp.bfloat16),
        pltpu.VMEM((steps, TILE, width), jnp.bfloat16),
        pltpu.VMEM(gate.shape, jnp.float32),
        pltpu.VMEM(up.shape, jnp.float32),
        pltpu.SemaphoreType.DMA((count,)),
        pltpu.SemaphoreType.DMA((steps,)),
        one,
        one,
    ]
    return run_kernel(
        body, (places, *cots, down_weight, gate, up), (out, out), scratch, "backward", 32
    )


def row_products(left, rights, tile, name, limit):
    (left_own, _), places = left, rights[0].get("places")
    rows, tall = left_own.shape
    sides = [side for right in rights for side in right["parts"]]
    flat = [*left, *(block for side in sides for block in side)]
    per_side = len(sides[0])
    wide = sides[0][0].shape[1]
    steps = tall // tile
    outs = len(rights)

    def body(places_ref, *refs):
        inputs, out_refs = refs[: len(flat)], refs[len(flat) : len(flat) + outs]
        lefts, right_bufs, stages, in_sem, out_sem = refs[len(flat) + outs :]
        loads = [
            pltpu.make_async_copy(inputs[r], lefts.at[r * rows : (r + 1) * rows, :], in_sem.at[r])
            for r in range(2)
        ]
        for k, source in enumerate(inputs[2:]):
            side, j = divmod(k, per_side)
            out, r = divmod(side, 2)
            target = right_bufs.at[out, r * rows : (r + 1) * rows, aligned(places_ref[j], wide)]
            loads.append(pltpu.make_async_copy(source, target, in_sem.at[2 + k]))
        for load in loads:
            load.start()
        for load in loads:
            load.wait()

        def store(out, i):
            return pltpu.make_async_copy(
                stages.at[out, i], out_refs[out].at[aligned(i, tile), :], out_sem.at[out, i]
            )

        for out in range(outs):

            def one_tile(i, _):
                stages[out, i] = lax.dot_general(
                    lefts[:, aligned(i, tile)],
                    right_bufs[out],
                    (((0,), (0,)), ((), ())),
                    preferred_element_type=jnp.float32,
                ).astype(jnp.bfloat16)
                store(out, i).start()
                return 0

            lax.fori_loop(0, steps, one_tile, 0)
        for out in range(outs):
            for i in range(steps):
                store(out, i).wait()

    width = wide * per_side
    outputs = (jax.ShapeDtypeStruct((tall, width), jnp.bfloat16),) * outs
    scratch = [
        pltpu.VMEM((2 * rows, tall), jnp.bfloat16),
        pltpu.VMEM((outs, 2 * rows, width), jnp.bfloat16),
        pltpu.VMEM((outs, steps, tile, width), jnp.bfloat16),
        pltpu.SemaphoreType.DMA((len(flat),)),
        pltpu.SemaphoreType.DMA((outs, steps)),
    ]
    if places is None:
        places = jnp.zeros((1,), jnp.int32)
    return run_kernel(body, (places, *flat), outputs, scratch, name, limit)


def tiled(
    teacher_hidden,
    teacher_gain,
    proj_weight,
    student_input,
    student_gain,
    gate_weight,
    up_weight,
    down_weight,
    block_order,
):
    eps = 1e-05
    bf16, f32 = jnp.bfloat16, jnp.float32
    core, section, tensor = (lax.axis_index(a) for a in ("split", "section", "tensor"))
    low, high = tensor & 1, tensor >> 1
    first = (("section", 0), ("tensor", 0))
    second = (("tensor", 0), ("section", 0))
    across = (("tensor", 1), ("tensor", 1))
    bit1 = jnp.where(core == 0, section, low)
    bit2 = jnp.where(core == 0, low, section)
    mask1 = jnp.where(core == 0, 1, 2)
    mask2 = 3 - mask1

    def partner(value):
        return swapped(value, "split", 0)

    rows, cols = student_input.shape
    own = jnp.concatenate(
        [student_input, jnp.broadcast_to(student_gain[None, :], (GAIN_ROWS, cols))], axis=0
    )
    far = phase_swap(own, across)
    near2 = phase_swap(own, second)
    near1 = phase_swap(own, first)
    near12 = phase_swap(near2, first)
    far2 = phase_swap(far, second)
    far1 = phase_swap(far, first)
    far12 = phase_swap(far2, first)
    me = tensor * 2 + section
    masks = (0, 4, mask2, mask1, 3, 4 ^ mask2, 4 ^ mask1, 7)
    block_own = bit1 * 2 + bit2
    block_other = bit2 * 2 + bit1
    info = jnp.stack(
        [me ^ m for m in masks] + [core, core * 4 + block_own, (1 - core) * 4 + block_other]
    ).astype(jnp.int32)
    width = cols * 8
    teacher_hidden, near2 = lax.optimization_barrier((teacher_hidden, near2))
    block, narrow = teacher_hidden.shape[0], teacher_hidden.shape[1] // 2
    leave = lax.dynamic_slice_in_dim(teacher_hidden, (1 - section) * narrow, narrow, 1)
    remain = lax.dynamic_slice_in_dim(teacher_hidden, section * narrow, narrow, 1)
    moved = jnp.concatenate([remain, swapped(leave, "section", 0)], axis=0)
    teach_local = teacher_hidden.astype(f32)
    total_sq = jnp.sum(teach_local * teach_local, axis=1)
    total_sq = total_sq + swapped(total_sq, "tensor", 0)
    total_sq = total_sq + swapped(total_sq, "tensor", 1)
    total_sq = jnp.concatenate([total_sq, swapped(total_sq, "section", 0)])
    picks = ((block_order // block) ^ section) * block + block_order % block
    piece_gain = lax.dynamic_slice_in_dim(teacher_gain, section * narrow, narrow, 0)
    chosen = picks[:, None] == jnp.arange(rows)[None, :]
    scaled = (moved.astype(f32) * piece_gain).astype(bf16)
    arranged = jnp.dot(chosen.astype(bf16), scaled, preferred_element_type=f32).astype(bf16)
    row_scale = jnp.sum(
        jnp.where(chosen, lax.rsqrt(total_sq / (narrow * 8) + eps)[None, :], 0.0), axis=1
    )
    row_scale = jnp.broadcast_to(row_scale[:, None], (rows, 128))
    target_own = jnp.dot(arranged, proj_weight, preferred_element_type=f32)
    target_other = jnp.dot(partner(arranged), proj_weight, preferred_element_type=f32)
    row_scale_other = partner(row_scale)
    far12, target_own, target_other = lax.optimization_barrier((far12, target_own, target_other))

    normed, normed_away, raw, raw_away, hidden, gate, up = forward(
        (own, far, near2, near1, near12, far2, far1, far12), gate_weight, up_weight, info, eps, width
    )
    hidden_other = partner(hidden)
    normed_other = partner(normed_away)
    raw_other = partner(raw_away)

    down_info = jnp.stack([core, bit1]).astype(jnp.int32)
    scale = 64.0 / (rows * 2)

    def cotangent_of(hidden_rows, target, scales, input_block):
        send, keep = project_down(hidden_rows, down_weight, target, scales, down_info)
        current = keep + phase_swap(send, first).astype(f32)
        half = current.shape[1] // 2
        send = lax.dynamic_slice_in_dim(current, (1 - bit2) * half, half, 1).astype(bf16)
        keep = lax.dynamic_slice_in_dim(current, bit2 * half, half, 1)
        current = keep + phase_swap(send, second).astype(f32)
        current = current + phase_swap(current.astype(bf16), across).astype(f32)
        piece = ((input_block.astype(f32) + current) * scale).astype(bf16)
        piece2 = phase_swap(piece, second)
        piece1 = phase_swap(piece, first)
        return piece, piece2, piece1, phase_swap(piece2, first)

    cots_own = cotangent_of(hidden, target_own, row_scale, raw)
    cots_other = cotangent_of(hidden_other, target_other, row_scale_other, raw_other)
    cots_got = tuple(partner(p) for p in cots_other)

    order = (0, 1, 2, 3)
    places_own = [block_own ^ m for m in order]
    places_got = [block_other ^ m for m in order]
    places = jnp.stack(
        [core * 4 + p for p in places_own] + [(1 - core) * 4 + p for p in places_got]
    ).astype(jnp.int32)
    d_gate, d_up = backward((*cots_own, *cots_got), places, down_weight, gate, up)
    d_gate_other, d_up_other = partner(d_gate), partner(d_up)
    (grad_down,) = row_products(
        (hidden, hidden_other),
        [{"parts": (cots_own, cots_other), "places": jnp.stack(places_own).astype(jnp.int32)}],
        TILE, "down_gradient", 24,
    )
    grad_gate, grad_up = row_products(
        (normed, normed_other),
        [{"parts": ((d_gate,), (d_gate_other,))}, {"parts": ((d_up,), (d_up_other,))}],
        2 * TILE, "input_gradients", 32,
    )
    return grad_gate, grad_up, grad_down


def fits_tiles(teacher_hidden, proj_weight, student_input, gate_weight):
    axes = tuple(lax.axis_size(a) for a in ("tensor", "section", "split"))
    rows, cols = student_input.shape
    return (
        axes == (4, 2, 2)
        and cols % TILE == 0
        and rows % TILE == 0
        and gate_weight.shape[1] % TILE == 0
        and proj_weight.shape[1] % (2 * TILE) == 0
        and teacher_hidden.shape[0] * 2 == rows
        and teacher_hidden.shape[1] % TILE == 0
    )


def on_device(*arrays):
    teacher_hidden, _, proj_weight, student_input, _, gate_weight = arrays[:6]
    plan = tiled if fits_tiles(teacher_hidden, proj_weight, student_input, gate_weight) else general
    return plan(*arrays)


def solution(mesh):
    placed = (
        P(("groups", "section", "split"), "tensor"),
        P("tensor"),
        P(("tensor", "section"), "split"),
        P(("groups", "split"), ("tensor", "section")),
        P(("tensor", "section")),
        P(None, ("tensor", "section")),
        P(None, ("tensor", "section")),
        P(("tensor", "section"), None),
        P(),
    )
    return jax.shard_map(
        on_device,
        mesh=mesh,
        in_specs=placed,
        out_specs=(
            P(("groups", "split"), ("tensor", "section")),
            P(("groups", "split"), ("tensor", "section")),
            P(("groups", "tensor", "section"), "split"),
        ),
        check_vma=False,
    )
```
